128 devices in a mesh: rows: 32 (over x, y, core), tok: 4 (over z).
Axes of the slice: x: 4, y: 4, z: 4, core: 2. Of those that a mesh axis runs over, the one named last changes fastest.
Arguments:
- pixels: bfloat16 [4096, 425, 512], P('rows', None, 'tok'), as said below
- scene_starts: int32 [4], replicated, may hold values from 0 to 4032, as said below
- owners: int32 [1024, 128], P('rows', 'tok'), may hold values from 0 to 31, as said below
- start_basis: float32 [425, 64], replicated, may hold values from -6 to 6
Outputs:
- tokens: bfloat16 [131072, 1024], P(('rows', 'tok'))
- noise_scores: bfloat16 [4096, 64, 512], P('rows', None, 'tok')
The draws below stay inside these ranges and needn't reach their ends.
Inputs may be any that keep to these rules, and one draw needn't show every extreme that they name: `scene_starts`: entry 0 is 0 and the entries rise strictly. `owners`: in each block of 32 x 128/4 patches every owner appears exactly 32 times. `pixels`: finite radiances; the scenes have a positive mean.
All inputs are finite; a program needn't handle non-finite values. Where the reference program divides by a largest or mean magnitude, that divisor is 1e-20 or more.
Results may differ from the reference program's by a relative error of at most 0.0068.
Values may be sent and summed in bfloat16 or wider, within the bound.
No kernel may reach another device: no remote copies, remote signals or barrier semaphores. Data moves between devices by JAX's collectives and lax.ppermute only.
A program may use at most 192 MiB of HBM per device.

```python
import jax
import jax.numpy as jnp
from jax import lax

B = 425
K = 64
PS = 4
NS_ITERS = 10
SUB_ITERS = 2
NSCENES = 4
RDEV = 128
CDEV = 128
IMG_ROWS = 4096
COLS = 512
PR = 1024
PC = 128
PATCHES = 131072
PER = 32
TOKLEN = 1024
N_ROWS = 32
N_TOK = 4


def draw_pixels(key, part):
    keys = jax.random.split(key, 7)
    half_rows = IMG_ROWS // 2
    shared = jax.random.normal(keys[0], (half_rows, B + 1, COLS), jnp.float32)
    speckle = jax.random.normal(keys[1], (IMG_ROWS, B + 1, COLS), jnp.float32)
    band_level = jax.random.uniform(keys[5], (B,), jnp.float32, 0.5, 2.0)
    shared = jnp.repeat(shared, 2, axis=0)
    signal_gain = jnp.exp(jax.random.uniform(keys[2], (B + 1,), jnp.float32, jnp.log(0.5), jnp.log(5.0)))
    noise_gain = jnp.exp(jax.random.uniform(keys[3], (B + 1,), jnp.float32, jnp.log(0.7), jnp.log(3.0)))
    raw = shared * signal_gain[None, :, None] + speckle * noise_gain[None, :, None]
    mixed = raw[:, :B, :] + 0.7 * raw[:, 1:, :]
    row_block = jnp.arange(IMG_ROWS, dtype=jnp.int32) // RDEV
    pairing = jax.random.permutation(keys[4], N_ROWS).astype(jnp.int32)
    band_slot = jnp.arange(B, dtype=jnp.int32) % N_ROWS
    boost = jnp.where(band_slot[None, :] == pairing[row_block][:, None], 4.0, 1.0)
    column_gain = jax.random.uniform(keys[6], (COLS,), jnp.float32, 0.6, 1.6)
    bright = 1.0 + 2.0 * jnp.arange(IMG_ROWS, dtype=jnp.float32) / jnp.float32(IMG_ROWS - 1)
    value = (mixed * boost[:, :, None] + band_level[None, :, None]) * column_gain[None, None, :]
    value = value * bright[:, None, None]
    return value.astype(jnp.bfloat16)


def draw_scene_starts(key, part):
    last_start = IMG_ROWS - RDEV // 2
    picked = jax.random.permutation(key, last_start - 1)[:NSCENES - 2] + 1
    picked = jnp.sort(picked.astype(jnp.int32))
    return jnp.concatenate([jnp.zeros((1,), jnp.int32), picked, jnp.full((1,), last_start, jnp.int32)])


def draw_owners(key, part):
    rows_per = RDEV // PS
    cols_per = CDEV // PS
    count = rows_per * cols_per
    base = jnp.arange(count, dtype=jnp.int32) % N_ROWS
    keys = jax.random.split(key, N_ROWS * N_TOK)
    shuffled = jax.vmap(lambda single: jax.random.permutation(single, base))(keys)
    shuffled = shuffled.reshape(N_ROWS, N_TOK, rows_per, cols_per).transpose(0, 2, 1, 3)
    return shuffled.reshape(PR, PC).astype(jnp.int32)


def gaussian(stream_key, shape, scale, most, kind=jnp.bfloat16):
    result = jax.random.normal(stream_key, shape, jnp.float32) * scale
    return jnp.minimum(jnp.maximum(result, -most), most).astype(kind)


def setup_inputs(seed: int = 0) -> dict:
    arg_keys = jax.random.split(jax.random.key(seed), 5)
    return {
        "pixels": draw_pixels(jax.random.fold_in(arg_keys[4], 71), 0),
        "scene_starts": draw_scene_starts(jax.random.fold_in(arg_keys[4], 71), 0),
        "owners": draw_owners(jax.random.fold_in(arg_keys[4], 71), 0),
        "start_basis": gaussian(arg_keys[3], (B, K), 1.0, 6.0, jnp.float32),
    }


def product(left, right):
    return jnp.dot(left, right, precision=lax.Precision.HIGHEST)

def whiten(noise_cov):
    width = noise_cov.shape[0]
    scale = jnp.max(lax.optimization_barrier(jnp.sum(jnp.abs(noise_cov), axis=1)))
    identity = jnp.eye(width, dtype=jnp.float32)
    upper = noise_cov / scale
    lower = identity
    for repeat in range(NS_ITERS):
        middle = 1.5 * identity - 0.5 * product(lower, upper)
        upper = product(upper, middle)
        lower = product(middle, lower)
    return lower / jnp.sqrt(scale)

def orthonormal(block):
    gram = product(block.T, block)
    factor = jnp.linalg.cholesky(gram)
    return lax.linalg.triangular_solve(factor, block, left_side=False, lower=True, transpose_a=True)

def reference(pixels, scene_starts, owners, start_basis):
    total_rows = IMG_ROWS
    row_index = jnp.arange(total_rows, dtype=jnp.int32)
    successor = row_index + 1
    starting = jnp.any(successor[:, None] == scene_starts[None, :], axis=1)
    valid = jnp.logical_and(successor < total_rows, jnp.logical_not(starting))
    following = jnp.concatenate([pixels[1:], jnp.zeros_like(pixels[:1])], axis=0)
    pixel_blocks = pixels.reshape(N_ROWS, RDEV, B, COLS)
    follow_blocks = following.reshape(N_ROWS, RDEV, B, COLS)
    valid_blocks = valid.reshape(N_ROWS, RDEV)

    def block_differ(block, ahead, keep):
        gap = block.astype(jnp.float32) - ahead.astype(jnp.float32)
        return jnp.where(keep[:, None, None], gap, 0.0).astype(jnp.bfloat16)

    def moments(items):
        block, ahead, keep = items
        differ = block_differ(block, ahead, keep).astype(jnp.float32)
        wide = block.astype(jnp.float32)
        noise_term = jnp.einsum('rbc,rec->be', differ, differ, precision=lax.Precision.HIGHEST)
        signal_term = jnp.einsum('rbc,rec->be', wide, wide, precision=lax.Precision.HIGHEST)
        return (noise_term, signal_term, lax.optimization_barrier(jnp.sum(wide, axis=(0, 2))))
    noise_terms, signal_terms, pixel_terms = lax.map(moments, (pixel_blocks, follow_blocks, valid_blocks))
    pixel_total = jnp.float32(IMG_ROWS * COLS)
    noise_cov = lax.optimization_barrier(jnp.sum(noise_terms, axis=0)) / jnp.float32(2 * (IMG_ROWS - NSCENES) * COLS)
    pixel_mean = lax.optimization_barrier(jnp.sum(pixel_terms, axis=0)) / pixel_total
    signal_cov = lax.optimization_barrier(jnp.sum(signal_terms, axis=0)) / pixel_total - pixel_mean[:, None] * pixel_mean[None, :]
    whitener = whiten(noise_cov)
    whitened = product(product(whitener, signal_cov), whitener)
    basis = orthonormal(start_basis)
    for repeat in range(SUB_ITERS):
        basis = orthonormal(product(whitened, basis))
    projector = product(whitener, basis).astype(jnp.bfloat16)
    wide_projector = projector.astype(jnp.float32)
    offset = product(pixel_mean, wide_projector)

    def project(items):
        block, ahead, keep = items
        differ = block_differ(block, ahead, keep).astype(jnp.float32)
        wide = block.astype(jnp.float32)
        comps = jnp.einsum('bk,rbc->rkc', wide_projector, wide, precision=lax.Precision.HIGHEST) - offset[None, :, None]
        scores = jnp.einsum('bk,rbc->rkc', wide_projector, differ, precision=lax.Precision.HIGHEST)
        return (comps.astype(jnp.bfloat16), scores.astype(jnp.bfloat16))
    comp_blocks, score_blocks = lax.map(project, (pixel_blocks, follow_blocks, valid_blocks))
    components = comp_blocks.reshape(IMG_ROWS, K, COLS)
    noise_scores = score_blocks.reshape(IMG_ROWS, K, COLS)
    patch_tokens = components.reshape(PR, PS, K, PC, PS).transpose(0, 3, 1, 4, 2).reshape(PR, PC, TOKLEN)
    rows_per = RDEV // PS
    cols_per = CDEV // PS
    block_tokens = patch_tokens.reshape(N_ROWS, rows_per, N_TOK, cols_per, TOKLEN).transpose(0, 2, 1, 3, 4)
    block_tokens = block_tokens.reshape(N_ROWS, N_TOK, rows_per * cols_per, TOKLEN)
    block_owners = owners.reshape(N_ROWS, rows_per, N_TOK, cols_per).transpose(0, 2, 1, 3)
    block_owners = block_owners.reshape(N_ROWS, N_TOK, rows_per * cols_per)
    order = jnp.argsort(block_owners, axis=-1, stable=True).astype(jnp.int32)
    ordered = jnp.take_along_axis(block_tokens, order[:, :, :, None], axis=2)
    ordered = ordered.reshape(N_ROWS, N_TOK, N_ROWS, PER, TOKLEN).transpose(2, 1, 0, 3, 4)
    tokens = ordered.reshape(PATCHES, TOKLEN)
    return (tokens, noise_scores)
```

```python
import functools

import jax
import jax.numpy as jnp
from jax import lax
from jax.experimental import pallas as pl
from jax.experimental.pallas import tpu as pltpu
from jax.sharding import PartitionSpec as P

B = 425
BP = 432
BW = 512
KC = 64
R = 16
OWN = 32
PATCHES = 1024
TILES = 128
F32 = jnp.float32
BF = jnp.bfloat16
NN = (((1,), (0,)), ((), ()))
NT = (((1,), (1,)), ((), ()))


def lower_gram(acc_ref, a):
    nt=(((1,),(1,)),((),()))
    g=lax.dot_general(a, a[0:256], nt, preferred_element_type=jnp.float32)
    h=lax.dot_general(a[256:432], a[256:432], nt, preferred_element_type=jnp.float32)
    acc_ref[0:432,:]+=g[:,0:128]
    acc_ref[432:736,:]+=g[128:432,128:256]
    acc_ref[736:912,:]+=h[:,0:128]
    acc_ref[912:960,0:48]+=h[128:176,128:176]

def noise_kernel(base_ref, starts_ref, x_ref, halo_ref, xt_ref, acc_ref, scr, prev, dbuf):
    s=pl.program_id(0); n=pl.num_programs(0)
    @pl.when(s==0)
    def _():
        acc_ref[...]=jnp.zeros_like(acc_ref)
        prev[...]=jnp.zeros_like(prev)
        scr[:,B*8:BP*8,:]=jnp.ones((2,(BP-B)*8,128),jnp.float32)
    def valid_after(row):
        nxt=base_ref[0]+row+1
        ok=nxt<4096
        for i in range(4):
            ok=jnp.logical_and(ok, nxt!=starts_ref[i])
        return jnp.logical_and(ok,row>=0)
    for g in range(2):
        scr[g,0:B*8,:]=x_ref[:,g*8:(g+1)*8,:].astype(jnp.float32).reshape(B*8,128)
    for r in range(R):
        cur=scr[r//8, pl.ds(r%8,BP,stride=8),:]
        before=prev[...] if r==0 else scr[(r-1)//8, pl.ds((r-1)%8,BP,stride=8),:]
        keep=valid_after(s*R+r-1)
        d=jnp.where(keep, before-cur, 0.0)
        dbuf[:,r*128:(r+1)*128]=d.astype(jnp.bfloat16)
        xt_ref[r]=cur.astype(jnp.bfloat16)
        if r==R-1: prev[...]=cur
    lower_gram(acc_ref, dbuf[...])
    @pl.when(s==n-1)
    def _():
        keep=valid_after(s*R+R-1)
        d=jnp.where(keep, prev[0:B]-halo_ref[0].astype(jnp.float32), 0.0)
        dd=jnp.concatenate([d,jnp.zeros((BP-B,128),jnp.float32)],0).astype(jnp.bfloat16)
        lower_gram(acc_ref, dd)

def noise_moments(pixels_t, halo, base, starts):
    return pl.pallas_call(noise_kernel,
      grid_spec=pltpu.PrefetchScalarGridSpec(num_scalar_prefetch=2, grid=(128//R,),
        in_specs=[pl.BlockSpec((B,R,128),lambda s,*_:(0,s,0)), pl.BlockSpec((1,B,128),lambda s,*_:(0,0,0))],
        out_specs=[pl.BlockSpec((R,BP,128),lambda s,*_:(s,0,0)), pl.BlockSpec((1024,128),lambda s,*_:(0,0))],
        scratch_shapes=[pltpu.VMEM((2,BP*8,128),jnp.float32), pltpu.VMEM((BP,128),jnp.float32), pltpu.VMEM((BP,R*128),jnp.bfloat16)]),
      out_shape=[jax.ShapeDtypeStruct((128,BP,128),jnp.bfloat16), jax.ShapeDtypeStruct((1024,128),jnp.float32)],
      compiler_params=pltpu.CompilerParams(vmem_limit_bytes=48<<20),
      cost_estimate=pl.CostEstimate(flops=6_000_000_000,bytes_accessed=30_000_000,transcendentals=0), name="noise_moments")(base,starts,pixels_t,halo)

def signal_kernel(xt_ref, acc_ref):
    @pl.when(pl.program_id(0)==0)
    def _(): acc_ref[...]=jnp.zeros_like(acc_ref)
    a=jnp.concatenate([xt_ref[r] for r in range(R)],axis=1)
    lower_gram(acc_ref,a)

def signal_moments(xt):
    return pl.pallas_call(signal_kernel, grid=(128//R,),
      in_specs=[pl.BlockSpec((R,BP,128),lambda s:(s,0,0))],
      out_specs=pl.BlockSpec((1024,128),lambda s:(0,0)),
      out_shape=jax.ShapeDtypeStruct((1024,128),jnp.float32),
      compiler_params=pltpu.CompilerParams(vmem_limit_bytes=48<<20),
      cost_estimate=pl.CostEstimate(flops=6_000_000_000,bytes_accessed=15_000_000,transcendentals=0), name="signal_moments")(xt)

def cut(x):
    hi=x.astype(BF)
    return hi,(x-hi.astype(F32)).astype(BF)

def times(a,b,dims=NN):
    (ah,al),(bh,bl)=a,b
    def mm(x,y): return lax.dot_general(x,y,dims,preferred_element_type=F32)
    return mm(ah,bh)+(mm(ah,bl)+mm(al,bh))

def unpacked(ref, full):
    starts=(0,432,736,912)
    for j in range(4):
        lo=starts[j]; rows=BP-128*j
        full[128*j:BP,128*j:128*(j+1)]=ref[lo:lo+rows,:]
    for j in range(4):
        for i in range(j+1,4):
            full[128*j:128*(j+1),128*i:128*(i+1)]=full[128*i:128*(i+1),128*j:128*(j+1)].T

def triangular_inverse(g):
    row=lax.broadcasted_iota(jnp.int32,(KC,2*KC),0); col=lax.broadcasted_iota(jnp.int32,(KC,2*KC),1)
    m=jnp.concatenate([g,jnp.zeros((KC,KC),F32)],axis=1)+jnp.where(col==row+KC,1.0,0.0)
    for j in range(KC):
        line=m[j:j+1,:]
        pivot=m[j:j+1,j:j+1]
        f=m[:,j:j+1]*(1.0/pivot)
        f=jnp.where(row>j,f,0.0)
        scaled=line*lax.rsqrt(pivot)
        m=jnp.where(row==j,scaled,m-f*line)
    return m[:,KC:]

def orthonormal(y):
    yc=cut(y)
    yt=y.T
    g=times(cut(yt),yc)
    li=triangular_inverse(g)
    return times(yc,cut(li),NT)

def put(ref,i,x):
    h,l=cut(x)
    ref[i,0,0:BP,:]=h; ref[i,1,0:BP,:]=l
def got(ref,i,rows=BW): return ref[i,0,0:rows,:],ref[i,1,0:rows,:]

def whiten_kernel(n_ref, w_ref, full, cuts, lf, *, norm, iters=10):
    full[...]=jnp.zeros_like(full)
    cuts[...]=jnp.zeros_like(cuts)
    unpacked(n_ref, full)
    row=lax.broadcasted_iota(jnp.int32,(BP,BW),0); col=lax.broadcasted_iota(jnp.int32,(BP,BW),1)
    inside=jnp.logical_and(row<B,col<B)
    cov=jnp.where(inside, full[0:BP,:]*(1.0/norm), 0.0)
    scale=jnp.max(jnp.sum(jnp.abs(cov),axis=1,keepdims=True),axis=0,keepdims=True)
    eye=jnp.where(jnp.logical_and(row==col,row<B),1.0,0.0)
    z=cov/scale
    full[0:BP,:]=z
    put(cuts,0,z)
    low=1.5*eye-0.5*z
    lf[...]=low
    put(cuts,1,low)
    for k in range(iters-1):
        w=1.5*z-0.5*times(got(cuts,0,BP),got(cuts,0))
        put(cuts,2,w)
        z=1.5*w-0.5*times(got(cuts,0,BP),got(cuts,2))
        full[0:BP,:]=z
        put(cuts,0,z)
        low=1.5*low-0.5*times(got(cuts,0,BP),got(cuts,1))
        put(cuts,1,low)
    w_ref[...]=low*lax.rsqrt(scale)

def whiten(tiles,norm):
    return pl.pallas_call(functools.partial(whiten_kernel,norm=norm),
      out_shape=jax.ShapeDtypeStruct((BP,BW),F32),
      scratch_shapes=[pltpu.VMEM((BW,BW),F32),pltpu.VMEM((3,2,BW,BW),BF),pltpu.VMEM((BP,BW),F32)],
      compiler_params=pltpu.CompilerParams(vmem_limit_bytes=40<<20),
      cost_estimate=pl.CostEstimate(flops=15_000_000_000,bytes_accessed=2_000_000,transcendentals=0),name="whiten")(tiles)

def start_kernel(b_ref,o_ref,pad):
    pad[...]=jnp.zeros_like(pad)
    pad[0:B,:]=b_ref[...]
    o_ref[...]=orthonormal(pad[...])

def start_orth(b):
    return pl.pallas_call(start_kernel,out_shape=jax.ShapeDtypeStruct((BP,KC),F32),scratch_shapes=[pltpu.VMEM((BP,KC),F32)],
      compiler_params=pltpu.CompilerParams(vmem_limit_bytes=40<<20),
      cost_estimate=pl.CostEstimate(flops=100_000_000,bytes_accessed=2_000_000,transcendentals=0),name="start_orth")(b)

def subspace_kernel(s_ref,w_ref,q_ref,pt_ref,full,cuts,thin,*,total):
    full[...]=jnp.zeros_like(full)
    cuts[...]=jnp.zeros_like(cuts)
    thin[...]=jnp.zeros_like(thin)
    unpacked(s_ref,full)
    row=lax.broadcasted_iota(jnp.int32,(BP,BW),0); col=lax.broadcasted_iota(jnp.int32,(BP,BW),1)
    inside=jnp.logical_and(row<B,col<B)
    mrow=full[B:B+1,:]*(1.0/total)
    mcol=full[0:BP,B:B+1]*(1.0/total)
    cov=jnp.where(inside,full[0:BP,:]*(1.0/total)-mcol*mrow,0.0)
    put(cuts,0,cov)
    put(cuts,1,w_ref[...])
    put(cuts,2,times(got(cuts,1,BP),got(cuts,0)))
    put(cuts,0,times(got(cuts,2,BP),got(cuts,1)))
    def thin_cut(x):
        h,l=cut(x); thin[0,0:BP,:]=h; thin[1,0:BP,:]=l
        return thin[0],thin[1]
    q=q_ref[...]
    for _ in range(2):
        q=orthonormal(times(got(cuts,0,BP),thin_cut(q)))
    p=times(got(cuts,1,BP),thin_cut(q)).astype(BF)
    pt=p.astype(F32).T
    off=-jnp.sum(pt*mrow[:,0:BP],axis=1,keepdims=True)
    lane=lax.broadcasted_iota(jnp.int32,(KC,BP),1)
    o1=off.astype(BF).astype(F32); o2=(off-o1).astype(BF).astype(F32); o3=off-o1-o2
    pt=jnp.where(lane<B,pt,jnp.where(lane==B,o1,jnp.where(lane==B+1,o2,jnp.where(lane==B+2,o3,0.0))))
    pt_ref[...]=pt.astype(BF)

def subspace(tiles,w,q,total):
    return pl.pallas_call(functools.partial(subspace_kernel,total=total),
      out_shape=jax.ShapeDtypeStruct((KC,BP),BF),
      scratch_shapes=[pltpu.VMEM((BW,BW),F32),pltpu.VMEM((3,2,BW,BW),BF),pltpu.VMEM((2,BW,KC),BF)],
      compiler_params=pltpu.CompilerParams(vmem_limit_bytes=40<<20),
      cost_estimate=pl.CostEstimate(flops=3_000_000_000,bytes_accessed=2_000_000,transcendentals=0),name="subspace")(tiles,w,q)

def order_kernel(o_ref, perm_ref):
    own=o_ref[...]
    hot=lax.broadcasted_iota(jnp.int32,(OWN,PATCHES),0)==own
    before=(lax.broadcasted_iota(jnp.int32,(PATCHES,PATCHES),0)<lax.broadcasted_iota(jnp.int32,(PATCHES,PATCHES),1))
    rank=lax.dot_general(hot.astype(F32).astype(BF),before.astype(F32).astype(BF),NN,preferred_element_type=F32)
    rank=jnp.sum(jnp.where(hot,rank,0.0),axis=0,keepdims=True)
    place=own*(PATCHES//OWN)+rank.astype(jnp.int32)
    perm_ref[...]=(lax.broadcasted_iota(jnp.int32,(PATCHES,PATCHES),0)==place).astype(F32).astype(BF)

def owner_order(own):
    return pl.pallas_call(order_kernel,out_shape=jax.ShapeDtypeStruct((PATCHES,PATCHES),BF),
      compiler_params=pltpu.CompilerParams(vmem_limit_bytes=40<<20),
      cost_estimate=pl.CostEstimate(flops=100_000_000,bytes_accessed=2_000_000,transcendentals=0),name="owner_order")(own)

def token_kernel(pt_ref,x_ref,perm_ref,out_ref,tok):
    s=pl.program_id(0); n=pl.num_programs(0)
    a=lax.broadcasted_iota(jnp.int32,(128,128),0); c=lax.broadcasted_iota(jnp.int32,(128,128),1)
    pick=((a%32)*4+a//32==c).astype(F32).astype(BF)
    pt=pt_ref[...]
    for p in range(R//4):
        ys=[]
        for h in range(2):
            r=4*p+2*h
            rhs=jnp.concatenate([x_ref[r],x_ref[r+1]],axis=1)
            y=lax.dot_general(pt,rhs,NN,preferred_element_type=F32).astype(BF)
            ys+=[y[:,0:128],y[:,128:256]]
        y=jnp.concatenate(ys,axis=0)
        t=lax.dot_general(pick,y,NT,preferred_element_type=F32)
        parts=[t[32*j:32*(j+1),64*i:64*(i+1)] for i in range(4) for j in range(4)]
        tok[pl.ds(pl.multiple_of(s*(R//4)*32+p*32,32),32),:]=jnp.concatenate(parts,axis=1).astype(BF)
    @pl.when(s==n-1)
    def _():
        for m in range(4):
            out_ref[256*m:256*(m+1),:]=lax.dot_general(perm_ref[256*m:256*(m+1),:],tok[...],NN,preferred_element_type=F32).astype(BF)

def token_blocks(pt,xt,perm):
    return pl.pallas_call(token_kernel,grid=(128//R,),
      in_specs=[pl.BlockSpec((KC,BP),lambda s:(0,0)),pl.BlockSpec((R,BP,128),lambda s:(s,0,0)),pl.BlockSpec((PATCHES,PATCHES),lambda s:(0,0))],
      out_specs=pl.BlockSpec((PATCHES,1024),lambda s:(0,0)),
      out_shape=jax.ShapeDtypeStruct((PATCHES,1024),BF),
      scratch_shapes=[pltpu.VMEM((PATCHES,1024),BF)],
      compiler_params=pltpu.CompilerParams(vmem_limit_bytes=48<<20),
      cost_estimate=pl.CostEstimate(flops=4_000_000_000,bytes_accessed=18_000_000,transcendentals=0),name="token_blocks")(pt,xt,perm)

def score_kernel(base_ref,starts_ref,pt_ref,x_ref,next_ref,halo_ref,out_ref):
    s=pl.program_id(0); n=pl.num_programs(0)
    pt=pt_ref[...]
    def differ(r):
        cur=x_ref[r].astype(F32)
        if r<R-1: ahead=x_ref[r+1].astype(F32)
        else:
            halo=jnp.concatenate([halo_ref[0].astype(F32),jnp.ones((BP-B,128),F32)],axis=0)
            ahead=jnp.where(s==n-1,halo,next_ref[0].astype(F32))
        nxt=base_ref[0]+s*R+r+1
        ok=nxt<4096
        for i in range(4): ok=jnp.logical_and(ok,nxt!=starts_ref[i])
        return jnp.where(ok,cur-ahead,0.0).astype(BF)
    for h in range(R//2):
        y=lax.dot_general(pt,jnp.concatenate([differ(2*h),differ(2*h+1)],axis=1),NN,preferred_element_type=F32).astype(BF)
        out_ref[2*h]=y[:,0:128]; out_ref[2*h+1]=y[:,128:256]

def scores(pt,xt,halo,base,starts):
    n=128//R
    return pl.pallas_call(score_kernel,
      grid_spec=pltpu.PrefetchScalarGridSpec(num_scalar_prefetch=2,grid=(n,),
        in_specs=[pl.BlockSpec((KC,BP),lambda s,*_:(0,0)),pl.BlockSpec((R,BP,128),lambda s,*_:(s,0,0)),
          pl.BlockSpec((1,BP,128),lambda s,*_:(jnp.minimum((s+1)*R,127),0,0)),pl.BlockSpec((1,B,128),lambda s,*_:(0,0,0))],
        out_specs=pl.BlockSpec((R,KC,128),lambda s,*_:(s,0,0))),
      out_shape=jax.ShapeDtypeStruct((128,KC,128),BF),
      compiler_params=pltpu.CompilerParams(vmem_limit_bytes=48<<20),
      cost_estimate=pl.CostEstimate(flops=4_000_000_000,bytes_accessed=18_000_000,transcendentals=0),name="noise_scores")(base,starts,pt,xt,xt,halo)


def local(pixels, scene_starts, owners, start_basis):
    rows = lax.axis_size("rows")
    cols = lax.axis_size("tok")
    local_rows = pixels.shape[0]
    both = ("rows", "tok")
    halo = lax.ppermute(pixels[0:1], "rows", [(r, r - 1) for r in range(1, rows)])
    base = (lax.axis_index("rows") * local_rows).astype(jnp.int32).reshape(1)
    total = float(rows * local_rows * cols * pixels.shape[2])
    norm = 2.0 * (rows * local_rows - scene_starts.shape[0]) * cols * pixels.shape[2]
    banded, noise_part = noise_moments(jnp.transpose(pixels, (1, 0, 2)), halo, base, scene_starts)
    noise_own = lax.all_to_all(noise_part.reshape(TILES, 8, 128), both, 0, 0, tiled=True).sum(axis=0)
    signal_part = signal_moments(banded)
    mixed = jnp.concatenate(
        [jnp.broadcast_to(noise_own, (TILES, 8, 128)), signal_part.reshape(TILES, 8, 128)], axis=1
    )
    mixed = lax.all_to_all(mixed, both, 0, 0, tiled=True)
    noise = mixed[:, 0:8].reshape(TILES * 8, 128)
    signal_own = mixed[:, 8:16].sum(axis=0)
    perm = owner_order(owners.reshape(1, PATCHES))
    basis = start_orth(start_basis)
    signal = lax.all_to_all(jnp.broadcast_to(signal_own, (TILES, 8, 128)), both, 0, 0, tiled=True)
    whitener = whiten(noise, norm)
    projector = subspace(signal.reshape(TILES * 8, 128), whitener, basis, total)
    outgoing = token_blocks(projector, banded, perm)
    arrived = lax.all_to_all(outgoing.reshape(OWN, PATCHES // OWN, 1024), "rows", 0, 0, tiled=True)
    noise_scores = scores(projector, banded, halo, base, scene_starts)
    return arrived.reshape(PATCHES, 1024), noise_scores


def solution(mesh):
    return jax.shard_map(
        local,
        mesh=mesh,
        in_specs=(P("rows", None, "tok"), P(), P("rows", "tok"), P()),
        out_specs=(P(("rows", "tok"), None), P("rows", None, "tok")),
        check_vma=False,
    )
```

```python
import functools

import jax
import jax.numpy as jnp
from jax import lax
from jax.experimental import pallas as pl
from jax.experimental.pallas import tpu as pltpu
from jax.sharding import PartitionSpec as P

B = 425
BP = 432
BW = 512
KC = 64
R = 16
OWN = 32
PATCHES = 1024
TILES = 128
F32 = jnp.float32
BF = jnp.bfloat16
NN = (((1,), (0,)), ((), ()))
NT = (((1,), (1,)), ((), ()))


def lower_gram(acc_ref, a):
    nt=(((1,),(1,)),((),()))
    g=lax.dot_general(a, a[0:256], nt, preferred_element_type=jnp.float32)
    h=lax.dot_general(a[256:432], a[256:432], nt, preferred_element_type=jnp.float32)
    acc_ref[0:432,:]+=g[:,0:128]
    acc_ref[432:736,:]+=g[128:432,128:256]
    acc_ref[736:912,:]+=h[:,0:128]
    acc_ref[912:960,0:48]+=h[128:176,128:176]

def kept(base_ref, starts_ref, row):
    nxt=base_ref[0]+row+1
    ok=jnp.logical_and(nxt<4096,row>=0)
    for i in range(4):
        ok=jnp.logical_and(ok, nxt!=starts_ref[i])
    return ok

CHUNK=48

def noise_kernel(base_ref, starts_ref, x_ref, xt_ref, acc_ref, scr, prev, even, odd):
    s=pl.program_id(0); n=pl.num_programs(0)
    @pl.when(s==0)
    def _():
        acc_ref[...]=jnp.zeros_like(acc_ref)
        prev[...]=jnp.zeros_like(prev)
        odd[...]=jnp.zeros_like(odd)
        scr[:,B*8:BP*8,:]=jnp.ones((4,(BP-B)*8,128),jnp.float32)
    for half,(dst,src) in enumerate(((even,odd),(odd,even))):
        lower_gram(acc_ref, src[...])
        keep=[kept(base_ref,starts_ref,s*2*R+half*R+r-1) for r in range(R)]
        for c in range(0,BP,CHUNK):
            top=min(c+CHUNK,B)
            before=prev[c:c+CHUNK,:]
            for g in range(2):
                scr[2*half+g,c*8:top*8,:]=x_ref[c:top,half*16+g*8:half*16+(g+1)*8,:].astype(jnp.float32).reshape((top-c)*8,128)
            for r in range(R):
                cur=scr[2*half+r//8, pl.ds(c*8+r%8,CHUNK,stride=8),:]
                dst[c:c+CHUNK,r*128:(r+1)*128]=jnp.where(keep[r], before-cur, 0.0).astype(jnp.bfloat16)
                xt_ref[half,c:c+CHUNK,r*128:(r+1)*128]=cur.astype(jnp.bfloat16)
                before=cur
            prev[c:c+CHUNK,:]=before
    @pl.when(s==n-1)
    def _():
        lower_gram(acc_ref, odd[...])

def noise_moments(pixels_t, base, starts):
    return pl.pallas_call(noise_kernel,
      grid_spec=pltpu.PrefetchScalarGridSpec(num_scalar_prefetch=2, grid=(128//(2*R),),
        in_specs=[pl.BlockSpec((B,2*R,128),lambda s,*_:(0,s,0))],
        out_specs=[pl.BlockSpec((2,BP,R*128),lambda s,*_:(s,0,0)), pl.BlockSpec((1024,128),lambda s,*_:(0,0))],
        scratch_shapes=[pltpu.VMEM((4,BP*8,128),jnp.float32), pltpu.VMEM((BP,128),jnp.float32)]+[pltpu.VMEM((BP,R*128),jnp.bfloat16)]*2),
      out_shape=[jax.ShapeDtypeStruct((128//R,BP,R*128),jnp.bfloat16), jax.ShapeDtypeStruct((1024,128),jnp.float32)],
      compiler_params=pltpu.CompilerParams(vmem_limit_bytes=48<<20),
      cost_estimate=pl.CostEstimate(flops=6_000_000_000,bytes_accessed=30_000_000,transcendentals=0), name="noise_moments")(base,starts,pixels_t)

def halo_kernel(base_ref, starts_ref, x_ref, halo_ref, part_ref, acc_ref):
    acc_ref[...]=part_ref[...]
    d=x_ref[0,0:B].astype(jnp.float32)-halo_ref[0].astype(jnp.float32)
    d=jnp.where(kept(base_ref,starts_ref,127), d, 0.0)
    d=jnp.concatenate([d,jnp.zeros((BP-B,128),jnp.float32)],0).astype(jnp.bfloat16)
    lower_gram(acc_ref, d)

def halo_moment(banded, halo, part, base, starts):
    return pl.pallas_call(halo_kernel,
      grid_spec=pltpu.PrefetchScalarGridSpec(num_scalar_prefetch=2, grid=(1,),
        in_specs=[pl.BlockSpec((1,BP,128),lambda s,*_:(128//R-1,0,R-1)), pl.BlockSpec((1,B,128),lambda s,*_:(0,0,0)), pl.BlockSpec((1024,128),lambda s,*_:(0,0))],
        out_specs=pl.BlockSpec((1024,128),lambda s,*_:(0,0))),
      out_shape=jax.ShapeDtypeStruct((1024,128),jnp.float32),
      compiler_params=pltpu.CompilerParams(vmem_limit_bytes=62<<20),
      cost_estimate=pl.CostEstimate(flops=50_000_000,bytes_accessed=1_300_000,transcendentals=0), name="halo_moment")(base,starts,banded,halo,part)

AHEAD=3

def signal_kernel(x_hbm, acc_ref, xbuf, sems):
    blocks=128//R
    def fetch(s): return pltpu.make_async_copy(x_hbm.at[s],xbuf.at[s],sems.at[s])
    for s in range(AHEAD): fetch(s).start()
    acc_ref[...]=jnp.zeros_like(acc_ref)
    @pl.loop(0,blocks)
    def _(s):
        fetch(s).wait()
        @pl.when(s+AHEAD<blocks)
        def _(): fetch(s+AHEAD).start()
        lower_gram(acc_ref,xbuf[s])

def signal_moments(xt):
    return pl.pallas_call(signal_kernel,
      in_specs=[pl.BlockSpec(memory_space=pl.ANY)],out_specs=pl.BlockSpec(memory_space=pltpu.VMEM),
      out_shape=jax.ShapeDtypeStruct((1024,128),jnp.float32),
      scratch_shapes=[pltpu.VMEM((128//R,BP,R*128),jnp.bfloat16),pltpu.SemaphoreType.DMA((128//R,))],
      compiler_params=pltpu.CompilerParams(vmem_limit_bytes=56<<20),
      cost_estimate=pl.CostEstimate(flops=6_000_000_000,bytes_accessed=15_000_000,transcendentals=0), name="signal_moments")(xt)

def cut(x):
    hi=x.astype(BF)
    return hi,(x-hi.astype(F32)).astype(BF)

def times(a,b,dims=NN):
    (ah,al),(bh,bl)=a,b
    def mm(x,y): return lax.dot_general(x,y,dims,preferred_element_type=F32)
    return mm(ah,bh)+(mm(ah,bl)+mm(al,bh))

def unpacked(ref, full):
    starts=(0,432,736,912)
    for j in range(4):
        lo=starts[j]; rows=BP-128*j
        full[128*j:BP,128*j:128*(j+1)]=ref[lo:lo+rows,:]
    for j in range(4):
        for i in range(j+1,4):
            full[128*j:128*(j+1),128*i:128*(i+1)]=full[128*i:128*(i+1),128*j:128*(j+1)].T

GROUP=8

def triangular_inverse(g):
    shape=(KC,2*KC)
    row=lax.broadcasted_iota(jnp.int32,shape,0); col=lax.broadcasted_iota(jnp.int32,shape,1)
    m=jnp.concatenate([g,jnp.zeros((KC,KC),F32)],axis=1)+jnp.where(col==row+KC,1.0,0.0)
    for j in range(0,KC,GROUP):
        lines=[m[j+a:j+a+1,:] for a in range(GROUP)]
        cols=[jnp.broadcast_to(m[:,j+a:j+a+1],shape) for a in range(GROUP)]
        roots=[]
        for a in range(GROUP):
            pivot=cols[a][j+a:j+a+1,:]
            inv=1.0/pivot
            roots.append(lax.rsqrt(pivot))
            for b in range(a+1,GROUP):
                f=cols[a][j+b:j+b+1,:]*inv
                lines[b]=lines[b]-f*lines[a]
                cols[b]=cols[b]-cols[a]*f
            cols[a]=cols[a]*inv
        below=row>=j+GROUP
        for a in range(GROUP): m=m-jnp.where(below,cols[a],0.0)*lines[a]
        for a in range(GROUP): m=jnp.where(row==j+a,lines[a]*roots[a],m)
    return m[:,KC:]

def orthonormal(y):
    yc=cut(y)
    yt=y.T
    g=times(cut(yt),yc)
    li=triangular_inverse(g)
    return times(yc,cut(li),NT)

def put(ref,i,x):
    h,l=cut(x)
    ref[i,0,0:BP,:]=h; ref[i,1,0:BP,:]=l
def got(ref,i,rows=BW): return ref[i,0,0:rows,:],ref[i,1,0:rows,:]

def times_symmetric(ref,i,j):
    a=got(ref,i,BP); b=got(ref,j)
    left=times(a,(b[0][:,0:256],b[1][:,0:256]))
    right=times((a[0][256:BP],a[1][256:BP]),(b[0][:,256:BW],b[1][:,256:BW]))
    corner=jnp.concatenate([left[256:BP],jnp.zeros((BW-BP,256),F32)],axis=0).T
    return jnp.concatenate([left,jnp.concatenate([corner,right],axis=0)],axis=1)

def whiten_kernel(n_ref, w_ref, full, cuts, *, norm, pairs):
    full[...]=jnp.zeros_like(full)
    cuts[...]=jnp.zeros_like(cuts)
    unpacked(n_ref, full)
    row=lax.broadcasted_iota(jnp.int32,(BP,BW),0); col=lax.broadcasted_iota(jnp.int32,(BP,BW),1)
    inside=jnp.logical_and(row<B,col<B)
    cov=jnp.where(inside, full[0:BP,:]*(1.0/norm), 0.0)
    scale=jnp.max(jnp.sum(jnp.abs(cov),axis=1,keepdims=True),axis=0,keepdims=True)
    eye=jnp.where(jnp.logical_and(row==col,row<B),1.0,0.0)
    z=cov/scale
    low=None
    for k in range(pairs):
        put(cuts,0,z)
        z2=times_symmetric(cuts,0,0)
        put(cuts,1,z2)
        put(cuts,2,0.0625*z2-0.5625*z)
        q=0.75*eye-2.4375*z+1.6875*z2+times_symmetric(cuts,1,2)
        put(cuts,1,q)
        if low is None: low=q+1.5*eye
        else:
            put(cuts,3,low)
            low=1.5*low+times_symmetric(cuts,1,3)
        if k<pairs-1:
            u=1.5*z+times_symmetric(cuts,0,1)
            put(cuts,2,u)
            z=1.5*u+times_symmetric(cuts,2,1)
    w_ref[...]=low*lax.rsqrt(scale)

def whiten(tiles,norm):
    return pl.pallas_call(functools.partial(whiten_kernel,norm=norm,pairs=5),
      out_shape=jax.ShapeDtypeStruct((BP,BW),F32),
      scratch_shapes=[pltpu.VMEM((BW,BW),F32),pltpu.VMEM((4,2,BW,BW),BF)],
      compiler_params=pltpu.CompilerParams(vmem_limit_bytes=24<<20),
      cost_estimate=pl.CostEstimate(flops=15_000_000_000,bytes_accessed=2_000_000,transcendentals=0),name="whiten")(tiles)

def start_kernel(b_ref,o_ref,pad):
    pad[...]=jnp.zeros_like(pad)
    pad[0:B,:]=b_ref[...]
    o_ref[...]=orthonormal(pad[...])

def start_orth(b):
    return pl.pallas_call(start_kernel,out_shape=jax.ShapeDtypeStruct((BP,KC),F32),scratch_shapes=[pltpu.VMEM((BP,KC),F32)],
      compiler_params=pltpu.CompilerParams(vmem_limit_bytes=40<<20),
      cost_estimate=pl.CostEstimate(flops=100_000_000,bytes_accessed=2_000_000,transcendentals=0),name="start_orth")(b)

def subspace_kernel(s_ref,w_ref,q_ref,pt_ref,full,cuts,thin,*,total):
    full[...]=jnp.zeros_like(full)
    cuts[...]=jnp.zeros_like(cuts)
    thin[...]=jnp.zeros_like(thin)
    unpacked(s_ref,full)
    row=lax.broadcasted_iota(jnp.int32,(BP,BW),0); col=lax.broadcasted_iota(jnp.int32,(BP,BW),1)
    inside=jnp.logical_and(row<B,col<B)
    mrow=full[B:B+1,:]*(1.0/total)
    mcol=full[0:BP,B:B+1]*(1.0/total)
    cov=jnp.where(inside,full[0:BP,:]*(1.0/total)-mcol*mrow,0.0)
    put(cuts,0,cov)
    put(cuts,1,w_ref[...])
    put(cuts,2,times(got(cuts,1,BP),got(cuts,0)))
    put(cuts,0,times(got(cuts,2,BP),got(cuts,1)))
    def thin_cut(x):
        h,l=cut(x); thin[0,0:BP,:]=h; thin[1,0:BP,:]=l
        return thin[0],thin[1]
    q=q_ref[...]
    for _ in range(2):
        q=orthonormal(times(got(cuts,0,BP),thin_cut(q)))
    p=times(got(cuts,1,BP),thin_cut(q)).astype(BF)
    pt=p.astype(F32).T
    off=-jnp.sum(pt*mrow[:,0:BP],axis=1,keepdims=True)
    lane=lax.broadcasted_iota(jnp.int32,(KC,BP),1)
    o1=off.astype(BF).astype(F32); o2=(off-o1).astype(BF).astype(F32); o3=off-o1-o2
    pt=jnp.where(lane<B,pt,jnp.where(lane==B,o1,jnp.where(lane==B+1,o2,jnp.where(lane==B+2,o3,0.0))))
    pt_ref[...]=pt.astype(BF)


def order_kernel(o_ref, perm_ref):
    own=o_ref[...]
    hot=lax.broadcasted_iota(jnp.int32,(OWN,PATCHES),0)==own
    before=(lax.broadcasted_iota(jnp.int32,(PATCHES,PATCHES),0)<lax.broadcasted_iota(jnp.int32,(PATCHES,PATCHES),1))
    rank=lax.dot_general(hot.astype(F32).astype(BF),before.astype(F32).astype(BF),NN,preferred_element_type=F32)
    rank=jnp.sum(jnp.where(hot,rank,0.0),axis=0,keepdims=True)
    place=own*(PATCHES//OWN)+rank.astype(jnp.int32)
    perm_ref[...]=(lax.broadcasted_iota(jnp.int32,(PATCHES,PATCHES),0)==place).astype(F32).astype(BF)

def owner_order(own):
    return pl.pallas_call(order_kernel,out_shape=jax.ShapeDtypeStruct((PATCHES,PATCHES),BF),
      compiler_params=pltpu.CompilerParams(vmem_limit_bytes=40<<20),
      cost_estimate=pl.CostEstimate(flops=100_000_000,bytes_accessed=2_000_000,transcendentals=0),name="owner_order")(own)

def project_kernel(s_ref,w_ref,q_ref,perm_ref,x_hbm,pt_ref,out_ref,full,cuts,thin,tok,xbuf,sems,*,total):
    blocks=128//R
    def fetch(s): return pltpu.make_async_copy(x_hbm.at[s],xbuf.at[s],sems.at[s])
    for s in range(blocks): fetch(s).start()
    subspace_kernel(s_ref,w_ref,q_ref,pt_ref,full,cuts,thin,total=total)
    a=lax.broadcasted_iota(jnp.int32,(128,128),0); c=lax.broadcasted_iota(jnp.int32,(128,128),1)
    pick=((a%32)*4+a//32==c).astype(F32).astype(BF)
    @pl.loop(0,blocks)
    def _(s):
        fetch(s).wait()
        pt=pt_ref[...]
        for p in range(R//4):
            ys=[]
            for h in range(2):
                r=4*p+2*h
                y=lax.dot_general(pt,xbuf[s,:,r*128:(r+2)*128],NN,preferred_element_type=F32).astype(BF)
                ys+=[y[:,0:128],y[:,128:256]]
            y=jnp.concatenate(ys,axis=0)
            t=lax.dot_general(pick,y,NT,preferred_element_type=F32)
            parts=[t[32*j:32*(j+1),64*i:64*(i+1)] for i in range(4) for j in range(4)]
            tok[pl.ds(pl.multiple_of(s*(R//4)*32+p*32,32),32),:]=jnp.concatenate(parts,axis=1).astype(BF)
    for m in range(4):
        out_ref[:,256*m:256*(m+1)]=lax.dot_general(perm_ref[...],tok[:,256*m:256*(m+1)],NN,preferred_element_type=F32).astype(BF)

def project(tiles,w,q,perm,xt,total):
    whole=pl.BlockSpec(memory_space=pltpu.VMEM)
    return pl.pallas_call(functools.partial(project_kernel,total=total),
      in_specs=[whole]*4+[pl.BlockSpec(memory_space=pl.ANY)],out_specs=[whole]*2,
      out_shape=[jax.ShapeDtypeStruct((KC,BP),BF),jax.ShapeDtypeStruct((PATCHES,1024),BF)],
      scratch_shapes=[pltpu.VMEM((BW,BW),F32),pltpu.VMEM((3,2,BW,BW),BF),pltpu.VMEM((2,BW,KC),BF),pltpu.VMEM((PATCHES,1024),BF),
        pltpu.VMEM((128//R,BP,R*128),BF),pltpu.SemaphoreType.DMA((128//R,))],
      compiler_params=pltpu.CompilerParams(vmem_limit_bytes=52<<20),
      cost_estimate=pl.CostEstimate(flops=8_000_000_000,bytes_accessed=18_000_000,transcendentals=0),name="project")(tiles,w,q,perm,xt)

def score_kernel(base_ref,starts_ref,pt_ref,x_ref,next_ref,halo_ref,out_ref):
    s=pl.program_id(0); n=pl.num_programs(0)
    pt=pt_ref[...]
    def differ(r):
        cur=x_ref[0,:,r*128:(r+1)*128].astype(F32)
        if r<R-1: ahead=x_ref[0,:,(r+1)*128:(r+2)*128].astype(F32)
        else:
            halo=jnp.concatenate([halo_ref[0].astype(F32),jnp.ones((BP-B,128),F32)],axis=0)
            ahead=jnp.where(s==n-1,halo,next_ref[0].astype(F32))
        return jnp.where(kept(base_ref,starts_ref,s*R+r),cur-ahead,0.0).astype(BF)
    for h in range(R//2):
        y=lax.dot_general(pt,jnp.concatenate([differ(2*h),differ(2*h+1)],axis=1),NN,preferred_element_type=F32).astype(BF)
        out_ref[2*h]=y[:,0:128]; out_ref[2*h+1]=y[:,128:256]

def scores(pt,xt,halo,base,starts):
    n=128//R
    return pl.pallas_call(score_kernel,
      grid_spec=pltpu.PrefetchScalarGridSpec(num_scalar_prefetch=2,grid=(n,),
        in_specs=[pl.BlockSpec((KC,BP),lambda s,*_:(0,0)),pl.BlockSpec((1,BP,R*128),lambda s,*_:(s,0,0)),
          pl.BlockSpec((1,BP,128),lambda s,*_:(jnp.minimum(s+1,128//R-1),0,0)),pl.BlockSpec((1,B,128),lambda s,*_:(0,0,0))],
        out_specs=pl.BlockSpec((R,KC,128),lambda s,*_:(s,0,0))),
      out_shape=jax.ShapeDtypeStruct((128,KC,128),BF),
      compiler_params=pltpu.CompilerParams(vmem_limit_bytes=63<<20),
      cost_estimate=pl.CostEstimate(flops=4_000_000_000,bytes_accessed=18_000_000,transcendentals=0),name="noise_scores")(base,starts,pt,xt,xt,halo)


def local(pixels, scene_starts, owners, start_basis):
    rows = lax.axis_size("rows")
    cols = lax.axis_size("tok")
    local_rows = pixels.shape[0]
    both = ("rows", "tok")
    halo = lax.ppermute(pixels[0:1], "rows", [(r, r - 1) for r in range(1, rows)])
    base = (lax.axis_index("rows") * local_rows).astype(jnp.int32).reshape(1)
    total = float(rows * local_rows * cols * pixels.shape[2])
    norm = 2.0 * (rows * local_rows - scene_starts.shape[0]) * cols * pixels.shape[2]
    banded, noise_part = noise_moments(jnp.transpose(pixels, (1, 0, 2)), base, scene_starts)
    noise_part = halo_moment(banded, halo, noise_part, base, scene_starts)
    noise_own = lax.all_to_all(noise_part.reshape(TILES, 8, 128), both, 0, 0, tiled=True).sum(axis=0)
    signal_part = signal_moments(banded)
    mixed = jnp.concatenate(
        [jnp.broadcast_to(noise_own, (TILES, 8, 128)), signal_part.reshape(TILES, 8, 128)], axis=1
    )
    mixed = lax.all_to_all(mixed, both, 0, 0, tiled=True)
    noise = mixed[:, 0:8].reshape(TILES * 8, 128)
    signal_own = mixed[:, 8:16].sum(axis=0)
    perm = owner_order(owners.reshape(1, PATCHES))
    basis = start_orth(start_basis)
    signal = lax.all_to_all(jnp.broadcast_to(signal_own, (TILES, 8, 128)), both, 0, 0, tiled=True)
    whitener = whiten(noise, norm)
    projector, outgoing = project(signal.reshape(TILES * 8, 128), whitener, basis, perm, banded, total)
    arrived = lax.all_to_all(outgoing.reshape(OWN, PATCHES // OWN, 1024), "rows", 0, 0, tiled=True)
    noise_scores = scores(projector, banded, halo, base, scene_starts)
    return arrived.reshape(PATCHES, 1024), noise_scores


def solution(mesh):
    return jax.shard_map(
        local,
        mesh=mesh,
        in_specs=(P("rows", None, "tok"), P(), P("rows", "tok"), P()),
        out_specs=(P(("rows", "tok"), None), P("rows", None, "tok")),
        check_vma=False,
    )
```

```python
import functools

import jax
import jax.numpy as jnp
from jax import lax
from jax.experimental import pallas as pl
from jax.experimental.pallas import tpu as pltpu
from jax.sharding import PartitionSpec as P

B = 425
BP = 432
BW = 512
KC = 64
R = 16
OWN = 32
PATCHES = 1024
TILES = 128
F32 = jnp.float32
BF = jnp.bfloat16
NN = (((1,), (0,)), ((), ()))
NT = (((1,), (1,)), ((), ()))


def lower_gram(acc_ref, a):
    nt=(((1,),(1,)),((),()))
    g=lax.dot_general(a, a[0:256], nt, preferred_element_type=jnp.float32)
    h=lax.dot_general(a[256:432], a[256:432], nt, preferred_element_type=jnp.float32)
    acc_ref[0:432,:]+=g[:,0:128]
    acc_ref[432:736,:]+=g[128:432,128:256]
    acc_ref[736:912,:]+=h[:,0:128]
    acc_ref[912:960,0:48]+=h[128:176,128:176]

def kept(base_ref, starts_ref, row):
    nxt=base_ref[0]+row+1
    ok=jnp.logical_and(nxt<4096,row>=0)
    for i in range(4):
        ok=jnp.logical_and(ok, nxt!=starts_ref[i])
    return ok

CHUNK=48

def noise_kernel(base_ref, starts_ref, x_ref, xt_ref, acc_ref, scr, prev, even, odd):
    s=pl.program_id(0); n=pl.num_programs(0)
    @pl.when(s==0)
    def _():
        acc_ref[...]=jnp.zeros_like(acc_ref)
        prev[...]=jnp.zeros_like(prev)
        odd[...]=jnp.zeros_like(odd)
        scr[:,B*8:BP*8,:]=jnp.ones((4,(BP-B)*8,128),jnp.float32)
    for half,(dst,src) in enumerate(((even,odd),(odd,even))):
        lower_gram(acc_ref, src[...])
        keep=[kept(base_ref,starts_ref,s*2*R+half*R+r-1) for r in range(R)]
        for c in range(0,BP,CHUNK):
            top=min(c+CHUNK,B)
            before=prev[c:c+CHUNK,:]
            for g in range(2):
                scr[2*half+g,c*8:top*8,:]=x_ref[c:top,half*16+g*8:half*16+(g+1)*8,:].astype(jnp.float32).reshape((top-c)*8,128)
            for r in range(R):
                cur=scr[2*half+r//8, pl.ds(c*8+r%8,CHUNK,stride=8),:]
                dst[c:c+CHUNK,r*128:(r+1)*128]=jnp.where(keep[r], before-cur, 0.0).astype(jnp.bfloat16)
                xt_ref[half,c:c+CHUNK,r*128:(r+1)*128]=cur.astype(jnp.bfloat16)
                before=cur
            prev[c:c+CHUNK,:]=before
    @pl.when(s==n-1)
    def _():
        lower_gram(acc_ref, odd[...])

def noise_moments(pixels_t, base, starts):
    return pl.pallas_call(noise_kernel,
      grid_spec=pltpu.PrefetchScalarGridSpec(num_scalar_prefetch=2, grid=(128//(2*R),),
        in_specs=[pl.BlockSpec((B,2*R,128),lambda s,*_:(0,s,0))],
        out_specs=[pl.BlockSpec((2,BP,R*128),lambda s,*_:(s,0,0)), pl.BlockSpec((1024,128),lambda s,*_:(0,0))],
        scratch_shapes=[pltpu.VMEM((4,BP*8,128),jnp.float32), pltpu.VMEM((BP,128),jnp.float32)]+[pltpu.VMEM((BP,R*128),jnp.bfloat16)]*2),
      out_shape=[jax.ShapeDtypeStruct((128//R,BP,R*128),jnp.bfloat16), jax.ShapeDtypeStruct((1024,128),jnp.float32)],
      compiler_params=pltpu.CompilerParams(vmem_limit_bytes=63<<20),
      cost_estimate=pl.CostEstimate(flops=6_000_000_000,bytes_accessed=30_000_000,transcendentals=0), name="noise_moments")(base,starts,pixels_t)

def halo_kernel(base_ref, starts_ref, x_ref, halo_ref, part_ref, acc_ref):
    acc_ref[...]=part_ref[...]
    d=x_ref[0,0:B].astype(jnp.float32)-halo_ref[0].astype(jnp.float32)
    d=jnp.where(kept(base_ref,starts_ref,127), d, 0.0)
    d=jnp.concatenate([d,jnp.zeros((BP-B,128),jnp.float32)],0).astype(jnp.bfloat16)
    lower_gram(acc_ref, d)

def halo_moment(banded, halo, part, base, starts):
    return pl.pallas_call(halo_kernel,
      grid_spec=pltpu.PrefetchScalarGridSpec(num_scalar_prefetch=2, grid=(1,),
        in_specs=[pl.BlockSpec((1,BP,128),lambda s,*_:(128//R-1,0,R-1)), pl.BlockSpec((1,B,128),lambda s,*_:(0,0,0)), pl.BlockSpec((1024,128),lambda s,*_:(0,0))],
        out_specs=pl.BlockSpec((1024,128),lambda s,*_:(0,0))),
      out_shape=jax.ShapeDtypeStruct((1024,128),jnp.float32),
      compiler_params=pltpu.CompilerParams(vmem_limit_bytes=53<<20),
      cost_estimate=pl.CostEstimate(flops=50_000_000,bytes_accessed=1_300_000,transcendentals=0), name="halo_moment")(base,starts,banded,halo,part)

AHEAD=3

def signal_kernel(x_hbm, acc_ref, xbuf, sems):
    blocks=128//R
    def fetch(s): return pltpu.make_async_copy(x_hbm.at[s],xbuf.at[s],sems.at[s])
    for s in range(AHEAD): fetch(s).start()
    acc_ref[...]=jnp.zeros_like(acc_ref)
    @pl.loop(0,blocks)
    def _(s):
        fetch(s).wait()
        @pl.when(s+AHEAD<blocks)
        def _(): fetch(s+AHEAD).start()
        lower_gram(acc_ref,xbuf[s])

def signal_moments(xt):
    return pl.pallas_call(signal_kernel,
      in_specs=[pl.BlockSpec(memory_space=pl.ANY)],out_specs=pl.BlockSpec(memory_space=pltpu.VMEM),
      out_shape=jax.ShapeDtypeStruct((1024,128),jnp.float32),
      scratch_shapes=[pltpu.VMEM((128//R,BP,R*128),jnp.bfloat16),pltpu.SemaphoreType.DMA((128//R,))],
      compiler_params=pltpu.CompilerParams(vmem_limit_bytes=53<<20),
      cost_estimate=pl.CostEstimate(flops=6_000_000_000,bytes_accessed=15_000_000,transcendentals=0), name="signal_moments")(xt)

def cut(x):
    hi=x.astype(BF)
    return hi,(x-hi.astype(F32)).astype(BF)

def times(a,b,dims=NN):
    (ah,al),(bh,bl)=a,b
    def mm(x,y): return lax.dot_general(x,y,dims,preferred_element_type=F32)
    return mm(ah,bh)+(mm(ah,bl)+mm(al,bh))

def unpacked(ref, full):
    starts=(0,432,736,912)
    for j in range(4):
        lo=starts[j]; rows=BP-128*j
        full[128*j:BP,128*j:128*(j+1)]=ref[lo:lo+rows,:]
    for j in range(4):
        for i in range(j+1,4):
            full[128*j:128*(j+1),128*i:128*(i+1)]=full[128*i:128*(i+1),128*j:128*(j+1)].T

GROUP=8

def triangular_inverse(g):
    shape=(KC,2*KC)
    row=lax.broadcasted_iota(jnp.int32,shape,0); col=lax.broadcasted_iota(jnp.int32,shape,1)
    m=jnp.concatenate([g,jnp.zeros((KC,KC),F32)],axis=1)+jnp.where(col==row+KC,1.0,0.0)
    for j in range(0,KC,GROUP):
        lines=[m[j+a:j+a+1,:] for a in range(GROUP)]
        cols=[jnp.broadcast_to(m[:,j+a:j+a+1],shape) for a in range(GROUP)]
        roots=[]
        for a in range(GROUP):
            pivot=cols[a][j+a:j+a+1,:]
            inv=1.0/pivot
            roots.append(lax.rsqrt(pivot))
            for b in range(a+1,GROUP):
                f=cols[a][j+b:j+b+1,:]*inv
                lines[b]=lines[b]-f*lines[a]
                cols[b]=cols[b]-cols[a]*f
            cols[a]=cols[a]*inv
        below=row>=j+GROUP
        for a in range(GROUP): m=m-jnp.where(below,cols[a],0.0)*lines[a]
        for a in range(GROUP): m=jnp.where(row==j+a,lines[a]*roots[a],m)
    return m[:,KC:]

def orthonormal(y):
    yc=cut(y)
    yt=y.T
    g=times(cut(yt),yc)
    li=triangular_inverse(g)
    return times(yc,cut(li),NT)

def put(ref,i,x):
    h,l=cut(x)
    ref[i,0,0:BP,:]=h; ref[i,1,0:BP,:]=l
def got(ref,i,rows=BW): return ref[i,0,0:rows,:],ref[i,1,0:rows,:]

def times_symmetric(ref,i,j):
    a=got(ref,i,BP); b=got(ref,j)
    left=times(a,(b[0][:,0:256],b[1][:,0:256]))
    right=times((a[0][256:BP],a[1][256:BP]),(b[0][:,256:BW],b[1][:,256:BW]))
    corner=jnp.concatenate([left[256:BP],jnp.zeros((BW-BP,256),F32)],axis=0).T
    return jnp.concatenate([left,jnp.concatenate([corner,right],axis=0)],axis=1)

def whiten_kernel(n_ref, w_ref, full, cuts, *, norm, pairs):
    full[...]=jnp.zeros_like(full)
    cuts[...]=jnp.zeros_like(cuts)
    unpacked(n_ref, full)
    row=lax.broadcasted_iota(jnp.int32,(BP,BW),0); col=lax.broadcasted_iota(jnp.int32,(BP,BW),1)
    inside=jnp.logical_and(row<B,col<B)
    cov=jnp.where(inside, full[0:BP,:]*(1.0/norm), 0.0)
    scale=jnp.max(jnp.sum(jnp.abs(cov),axis=1,keepdims=True),axis=0,keepdims=True)
    eye=jnp.where(jnp.logical_and(row==col,row<B),1.0,0.0)
    z=cov/scale
    low=None
    for k in range(pairs):
        put(cuts,0,z)
        z2=times_symmetric(cuts,0,0)
        put(cuts,1,z2)
        put(cuts,2,0.0625*z2-0.5625*z)
        q=0.75*eye-2.4375*z+1.6875*z2+times_symmetric(cuts,1,2)
        put(cuts,1,q)
        if low is None: low=q+1.5*eye
        else:
            put(cuts,3,low)
            low=1.5*low+times_symmetric(cuts,1,3)
        if k<pairs-1:
            u=1.5*z+times_symmetric(cuts,0,1)
            put(cuts,2,u)
            z=1.5*u+times_symmetric(cuts,2,1)
    w_ref[...]=low*lax.rsqrt(scale)

def whiten(tiles,norm):
    return pl.pallas_call(functools.partial(whiten_kernel,norm=norm,pairs=5),
      out_shape=jax.ShapeDtypeStruct((BP,BW),F32),
      scratch_shapes=[pltpu.VMEM((BW,BW),F32),pltpu.VMEM((4,2,BW,BW),BF)],
      compiler_params=pltpu.CompilerParams(vmem_limit_bytes=24<<20),
      cost_estimate=pl.CostEstimate(flops=15_000_000_000,bytes_accessed=2_000_000,transcendentals=0),name="whiten")(tiles)

def start_kernel(b_ref,o_ref,pad):
    pad[...]=jnp.zeros_like(pad)
    pad[0:B,:]=b_ref[...]
    o_ref[...]=orthonormal(pad[...])

def start_orth(b):
    return pl.pallas_call(start_kernel,out_shape=jax.ShapeDtypeStruct((BP,KC),F32),scratch_shapes=[pltpu.VMEM((BP,KC),F32)],
      compiler_params=pltpu.CompilerParams(vmem_limit_bytes=40<<20),
      cost_estimate=pl.CostEstimate(flops=100_000_000,bytes_accessed=2_000_000,transcendentals=0),name="start_orth")(b)

def subspace_kernel(s_ref,w_ref,q_ref,pt_ref,full,cuts,thin,*,total):
    full[...]=jnp.zeros_like(full)
    cuts[...]=jnp.zeros_like(cuts)
    thin[...]=jnp.zeros_like(thin)
    unpacked(s_ref,full)
    row=lax.broadcasted_iota(jnp.int32,(BP,BW),0); col=lax.broadcasted_iota(jnp.int32,(BP,BW),1)
    inside=jnp.logical_and(row<B,col<B)
    mrow=full[B:B+1,:]*(1.0/total)
    mcol=full[0:BP,B:B+1]*(1.0/total)
    cov=jnp.where(inside,full[0:BP,:]*(1.0/total)-mcol*mrow,0.0)
    put(cuts,0,cov)
    put(cuts,1,w_ref[...])
    put(cuts,2,times(got(cuts,1,BP),got(cuts,0)))
    put(cuts,0,times(got(cuts,2,BP),got(cuts,1)))
    def thin_cut(x):
        h,l=cut(x); thin[0,0:BP,:]=h; thin[1,0:BP,:]=l
        return thin[0],thin[1]
    q=q_ref[...]
    for _ in range(2):
        q=orthonormal(times(got(cuts,0,BP),thin_cut(q)))
    p=times(got(cuts,1,BP),thin_cut(q)).astype(BF)
    pt=p.astype(F32).T
    off=-jnp.sum(pt*mrow[:,0:BP],axis=1,keepdims=True)
    lane=lax.broadcasted_iota(jnp.int32,(KC,BP),1)
    o1=off.astype(BF).astype(F32); o2=(off-o1).astype(BF).astype(F32); o3=off-o1-o2
    pt=jnp.where(lane<B,pt,jnp.where(lane==B,o1,jnp.where(lane==B+1,o2,jnp.where(lane==B+2,o3,0.0))))
    pt_ref[...]=pt.astype(BF)


def order_kernel(o_ref, perm_ref):
    own=o_ref[...]
    hot=lax.broadcasted_iota(jnp.int32,(OWN,PATCHES),0)==own
    before=(lax.broadcasted_iota(jnp.int32,(PATCHES,PATCHES),0)<lax.broadcasted_iota(jnp.int32,(PATCHES,PATCHES),1))
    rank=lax.dot_general(hot.astype(F32).astype(BF),before.astype(F32).astype(BF),NN,preferred_element_type=F32)
    rank=jnp.sum(jnp.where(hot,rank,0.0),axis=0,keepdims=True)
    place=own*(PATCHES//OWN)+rank.astype(jnp.int32)
    perm_ref[...]=(lax.broadcasted_iota(jnp.int32,(PATCHES,PATCHES),0)==place).astype(F32).astype(BF)

def owner_order(own):
    return pl.pallas_call(order_kernel,out_shape=jax.ShapeDtypeStruct((PATCHES,PATCHES),BF),
      compiler_params=pltpu.CompilerParams(vmem_limit_bytes=40<<20),
      cost_estimate=pl.CostEstimate(flops=100_000_000,bytes_accessed=2_000_000,transcendentals=0),name="owner_order")(own)

def project_kernel(s_ref,w_ref,q_ref,perm_ref,x_hbm,pt_ref,out_ref,full,cuts,thin,tok,xbuf,sems,*,total):
    blocks=128//R
    def fetch(s): return pltpu.make_async_copy(x_hbm.at[s],xbuf.at[s],sems.at[s])
    for s in range(blocks): fetch(s).start()
    subspace_kernel(s_ref,w_ref,q_ref,pt_ref,full,cuts,thin,total=total)
    a=lax.broadcasted_iota(jnp.int32,(64,256),0); c=lax.broadcasted_iota(jnp.int32,(64,256),1)
    pick=((a%32)*4+a//32*2+c//128==c%128).astype(F32).astype(BF)
    none=jnp.zeros((KC,128),BF)
    @pl.loop(0,blocks)
    def _(s):
        fetch(s).wait()
        pt=pt_ref[...]
        for p in range(R//4):
            parts=[]
            for h in range(2):
                r=4*p+2*h
                y=lax.dot_general(pt,xbuf[s,:,r*128:(r+2)*128],NN,preferred_element_type=F32).astype(BF)
                rows=[]
                for i in range(2):
                    yi=y[:,128*i:128*(i+1)]
                    rows+=[jnp.concatenate([yi,none],axis=1),jnp.concatenate([none,yi],axis=1)]
                t=lax.dot_general(pick,jnp.concatenate(rows,axis=0),NT,preferred_element_type=F32)
                parts+=[t[32*g:32*(g+1),128*i:128*(i+1)] for i in range(2) for g in range(2)]
            tok[pl.ds(pl.multiple_of(s*(R//4)*32+p*32,32),32),:]=jnp.concatenate(parts,axis=1).astype(BF)
    for m in range(4):
        out_ref[:,256*m:256*(m+1)]=lax.dot_general(perm_ref[...],tok[:,256*m:256*(m+1)],NN,preferred_element_type=F32).astype(BF)

def project(tiles,w,q,perm,xt,total):
    whole=pl.BlockSpec(memory_space=pltpu.VMEM)
    return pl.pallas_call(functools.partial(project_kernel,total=total),
      in_specs=[whole]*4+[pl.BlockSpec(memory_space=pl.ANY)],out_specs=[whole]*2,
      out_shape=[jax.ShapeDtypeStruct((KC,BP),BF),jax.ShapeDtypeStruct((PATCHES,1024),BF)],
      scratch_shapes=[pltpu.VMEM((BW,BW),F32),pltpu.VMEM((3,2,BW,BW),BF),pltpu.VMEM((2,BW,KC),BF),pltpu.VMEM((PATCHES,1024),BF),
        pltpu.VMEM((128//R,BP,R*128),BF),pltpu.SemaphoreType.DMA((128//R,))],
      compiler_params=pltpu.CompilerParams(vmem_limit_bytes=52<<20),
      cost_estimate=pl.CostEstimate(flops=8_000_000_000,bytes_accessed=18_000_000,transcendentals=0),name="project")(tiles,w,q,perm,xt)

def score_kernel(base_ref,starts_ref,pt_ref,x_ref,next_ref,halo_ref,out_ref):
    s=pl.program_id(0); n=pl.num_programs(0)
    pt=pt_ref[...]
    def differ(r):
        cur=x_ref[0,:,r*128:(r+1)*128].astype(F32)
        if r<R-1: ahead=x_ref[0,:,(r+1)*128:(r+2)*128].astype(F32)
        else:
            halo=jnp.concatenate([halo_ref[0].astype(F32),jnp.ones((BP-B,128),F32)],axis=0)
            ahead=jnp.where(s==n-1,halo,next_ref[0].astype(F32))
        return jnp.where(kept(base_ref,starts_ref,s*R+r),cur-ahead,0.0).astype(BF)
    for h in range(R//2):
        y=lax.dot_general(pt,jnp.concatenate([differ(2*h),differ(2*h+1)],axis=1),NN,preferred_element_type=F32).astype(BF)
        out_ref[2*h]=y[:,0:128]; out_ref[2*h+1]=y[:,128:256]

def scores(pt,xt,halo,base,starts):
    n=128//R
    return pl.pallas_call(score_kernel,
      grid_spec=pltpu.PrefetchScalarGridSpec(num_scalar_prefetch=2,grid=(n,),
        in_specs=[pl.BlockSpec((KC,BP),lambda s,*_:(0,0)),pl.BlockSpec((1,BP,R*128),lambda s,*_:(s,0,0)),
          pl.BlockSpec((1,BP,128),lambda s,*_:(jnp.minimum(s+1,128//R-1),0,0)),pl.BlockSpec((1,B,128),lambda s,*_:(0,0,0))],
        out_specs=pl.BlockSpec((R,KC,128),lambda s,*_:(s,0,0))),
      out_shape=jax.ShapeDtypeStruct((128,KC,128),BF),
      compiler_params=pltpu.CompilerParams(vmem_limit_bytes=48<<20),
      cost_estimate=pl.CostEstimate(flops=4_000_000_000,bytes_accessed=18_000_000,transcendentals=0),name="noise_scores")(base,starts,pt,xt,xt,halo)


def local(pixels, scene_starts, owners, start_basis):
    rows = lax.axis_size("rows")
    cols = lax.axis_size("tok")
    local_rows = pixels.shape[0]
    both = ("rows", "tok")
    halo = lax.ppermute(pixels[0:1], "rows", [(r, r - 1) for r in range(1, rows)])
    base = (lax.axis_index("rows") * local_rows).astype(jnp.int32).reshape(1)
    total = float(rows * local_rows * cols * pixels.shape[2])
    norm = 2.0 * (rows * local_rows - scene_starts.shape[0]) * cols * pixels.shape[2]
    banded, noise_part = noise_moments(jnp.transpose(pixels, (1, 0, 2)), base, scene_starts)
    noise_part = halo_moment(banded, halo, noise_part, base, scene_starts)
    noise_own = lax.all_to_all(noise_part.reshape(TILES, 8, 128), both, 0, 0, tiled=True).sum(axis=0)
    signal_part = signal_moments(banded)
    mixed = jnp.concatenate(
        [jnp.broadcast_to(noise_own, (TILES, 8, 128)), signal_part.reshape(TILES, 8, 128)], axis=1
    )
    mixed = lax.all_to_all(mixed, both, 0, 0, tiled=True)
    noise = mixed[:, 0:8].reshape(TILES * 8, 128)
    signal_own = mixed[:, 8:16].sum(axis=0)
    perm = owner_order(owners.reshape(1, PATCHES))
    basis = start_orth(start_basis)
    signal = lax.all_to_all(jnp.broadcast_to(signal_own, (TILES, 8, 128)), both, 0, 0, tiled=True)
    whitener = whiten(noise, norm)
    projector, outgoing = project(signal.reshape(TILES * 8, 128), whitener, basis, perm, banded, total)
    arrived = lax.all_to_all(outgoing.reshape(OWN, PATCHES // OWN, 1024), "rows", 0, 0, tiled=True)
    noise_scores = scores(projector, banded, halo, base, scene_starts)
    return arrived.reshape(PATCHES, 1024), noise_scores


def solution(mesh):
    return jax.shard_map(
        local,
        mesh=mesh,
        in_specs=(P("rows", None, "tok"), P(), P("rows", "tok"), P()),
        out_specs=(P(("rows", "tok"), None), P("rows", None, "tok")),
        check_vma=False,
    )
```
